256 devices in a mesh: table: 64 (over y, z, core), rep: 4 (over x).
Axes of the slice: x: 4, y: 4, z: 8, core: 2. Of those that a mesh axis runs over, the one named last changes fastest.
Arguments:
- embedding_table: float32 [131072, 128], P('table'), may hold values from -1.8 to 1.8
- row_history: float32 [131072], P('table'), may hold values from 0.5 to 4
- hot_table: float32 [262144, 128], P('table'), may hold values from -1.8 to 1.8
- hot_history: float32 [262144], P('table'), may hold values from 10 to 1000
- hot_owner: int32 [1], replicated, may hold values from 0 to 63
- cold_index: int32 [4, 4096, 256], P('rep', 'table'), may hold values from 0 to 2047
- cold_counts: int32 [4, 4096], P('rep', 'table'), may hold values from 1 to 256, as said below
- cold_bags: int32 [4, 4096, 256], P('rep', 'table'), may hold values from 0 to 255
- hot_index: int32 [4, 131072], P('rep', 'table'), may hold values from 0 to 4095
- hot_bags: int32 [4, 131072], P('rep', 'table'), may hold values from 0 to 255
- pooled_grad: bfloat16 [4, 16384, 128], P('rep', 'table'), may hold values from -6 to 6
Outputs:
- pooled_bags: bfloat16 [4, 16384, 128], P('rep', 'table')
- next_table: float32 [131072, 128], P('table')
- next_history: float32 [131072], P('table')
- next_hot: float32 [262144, 128], P('table')
- next_squares: float32 [262144], P('table')
The draws below stay inside these ranges and needn't reach their ends.
Inputs may be any that keep to these rules, and one draw needn't show every extreme that they name: `cold_counts`: slots of a request list past its count are padding. In every draw some owner receives 256 live slots from every device of every replica, and some lists are full.
All inputs are finite; a program needn't handle non-finite values.
Results may differ from the reference program's by a relative error of at most 0.0028.
The reference program's roundings to bfloat16 on the way (of `pulled` and `hot_block`) count: a program that leaves them out, or rounds other values in their place, can miss the bound.
Values may be sent and summed in bfloat16 or wider, within the bound.
No kernel may reach another device: no remote copies, remote signals or barrier semaphores. Data moves between devices by JAX's collectives and lax.ppermute only.
A program may use at most 64 MiB of HBM per device.

```python
import math
import jax
import jax.numpy as jnp
import numpy as np
from jax import lax

D = 128
ROWS_DEV = 2048
SLOTS = 256
B_DEV = 256
HOT = 4096
HOT_LOOK = 2048
SHARDS = 64
REPLICAS = 4
ROWS = 131072


def draw_cold_counts(key, part):
    heavy_key, base_key, full_key = jax.random.split(key, 3)
    heavy_factor = jax.random.randint(heavy_key, (SHARDS,), 1, 5)
    base_counts = jax.random.randint(base_key, (REPLICAS, SHARDS, SHARDS), 1, SLOTS // 4 + 1)
    slot_counts = jnp.minimum(base_counts * heavy_factor[None, None, :], SLOTS)
    full_owner = jax.random.randint(full_key, (), 0, SHARDS)
    owners = jnp.arange(SHARDS)[None, None, :]
    slot_counts = jnp.where(owners == full_owner, SLOTS, slot_counts)
    return slot_counts.reshape(REPLICAS, SHARDS * SHARDS).astype(jnp.int32)


def set_ends(entries, stream_key, smallest, top_value):
    spot = [jax.random.randint(jax.random.fold_in(stream_key, axis), (), 0, length) for axis, length in enumerate(entries.shape)]
    widest = entries.shape.index(max(entries.shape))
    neighbour = spot[:widest] + [(spot[widest] + 1) % entries.shape[widest]] + spot[widest + 1:]
    return entries.at[tuple(spot)].set(smallest).at[tuple(neighbour)].set(top_value)


def block_scale(key, dims, shards, smallest, largest):
    gain = 1.0
    for dim, blocks in shards:
        draws = jax.random.uniform(jax.random.fold_in(jax.random.fold_in(key, 6), dim), (blocks,), jnp.float32, smallest / len(shards), largest / len(shards))
        gain = gain * jnp.repeat(jnp.exp(draws), dims[dim] // blocks).reshape((-1,) + (1,) * (len(dims) - 1 - dim))
    return gain


def rank_table(amount, lean):
    portions = [(1 << 20) // math.isqrt(grade ** lean) + 1 for grade in range(1, amount + 1)]
    deviation = 1 + sum(portions) // (1 << 30)
    return np.cumsum(np.array([max(1, weight // deviation) for weight in portions]))


def ranked_ids(key, shape, amount, slope):
    grid = rank_table(amount, slope)
    pick = jax.random.randint(jax.random.fold_in(key, 1), shape, 0, int(grid[amount - 1]))
    grade = jnp.searchsorted(jnp.asarray(grid, jnp.int32), pick, side="right")
    return jax.random.permutation(jax.random.fold_in(key, 2), amount)[grade].astype(jnp.int32)


def noise(rng, shape, deviation, reach, pieces=(), held_as=jnp.bfloat16):
    factor_of = block_scale(rng, shape, pieces, -0.22, 0.18) if pieces else 1.0
    result = jax.random.normal(rng, shape, jnp.float32) * deviation * factor_of
    return jnp.minimum(jnp.maximum(result, -reach), reach).astype(held_as)


def setup_inputs(seed: int = 0) -> dict:
    seeds = jax.random.split(jax.random.key(seed), 12)
    return {
        "embedding_table": noise(seeds[0], (ROWS, D), 0.3, 1.8, ((0, 64),), jnp.float32),
        "row_history": jnp.clip(jnp.exp(math.log(4.0) - 2.0794415 * jax.random.uniform(seeds[1], (ROWS,), jnp.float32) ** block_scale(seeds[1], (ROWS,), ((0, 64),), -0.2, 0.2)), 0.5, 4.0),
        "hot_table": noise(seeds[2], (SHARDS * HOT, D), 0.3, 1.8, ((0, 64),), jnp.float32),
        "hot_history": jnp.clip(jnp.exp(math.log(1000.0) - 4.6051702 * jax.random.uniform(seeds[3], (SHARDS * HOT,), jnp.float32) ** block_scale(seeds[3], (SHARDS * HOT,), ((0, 64),), -0.2, 0.2)), 10.0, 1000.0),
        "hot_owner": jax.random.randint(seeds[4], (1,), 0, SHARDS).astype(jnp.int32),
        "cold_index": set_ends(jax.random.randint(seeds[5], (REPLICAS, SHARDS * SHARDS, SLOTS), 0, ROWS_DEV), jax.random.fold_in(seeds[5], 1), 0, ROWS_DEV - 1).astype(jnp.int32),
        "cold_counts": draw_cold_counts(jax.random.fold_in(seeds[11], 71), 0),
        "cold_bags": set_ends(jax.random.randint(seeds[7], (REPLICAS, SHARDS * SHARDS, SLOTS), 0, B_DEV), jax.random.fold_in(seeds[7], 1), 0, B_DEV - 1).astype(jnp.int32),
        "hot_index": set_ends(ranked_ids(seeds[8], (REPLICAS, SHARDS * HOT_LOOK), HOT, 2), jax.random.fold_in(seeds[8], 3), 0, HOT - 1).astype(jnp.int32),
        "hot_bags": set_ends(jax.random.randint(seeds[9], (REPLICAS, SHARDS * HOT_LOOK), 0, B_DEV), jax.random.fold_in(seeds[9], 1), 0, B_DEV - 1).astype(jnp.int32),
        "pooled_grad": noise(seeds[10], (REPLICAS, SHARDS * B_DEV, D), 1.0, 6.0, ((0, 4), (1, 64))),
    }


learn_rate = 0.1
epsilon = 1e-08

def adagrad_rows(weights, history, gradient):
    updated = history + lax.optimization_barrier(jnp.mean(gradient * gradient, axis=1))
    return (weights - learn_rate * gradient / (jnp.sqrt(updated)[:, None] + epsilon), updated)

def reference(embedding_table, row_history, hot_table, hot_history, hot_owner, cold_index, cold_counts, cold_bags, hot_index, hot_bags, pooled_grad):
    owner_index = hot_owner[0].astype(jnp.int32)
    owner_start = (owner_index * HOT).astype(jnp.int32)
    owner_rows = lax.dynamic_slice_in_dim(hot_table, owner_start, HOT, 0)
    hot_block = lax.optimization_barrier(owner_rows.astype(jnp.bfloat16))
    offsets = (jnp.arange(SHARDS, dtype=jnp.int32) * ROWS_DEV)[:, None]
    columns = jnp.arange(SLOTS, dtype=jnp.int32)[None, :]
    device_count = REPLICAS * SHARDS
    item_list = (cold_index.reshape(device_count, SHARDS, SLOTS), cold_counts.reshape(device_count, SHARDS), cold_bags.reshape(device_count, SHARDS * SLOTS), hot_index.reshape(device_count, HOT_LOOK), hot_bags.reshape(device_count, HOT_LOOK), pooled_grad.reshape(device_count, B_DEV, D))

    def visit(carried, item_data):
        dense_grad, hot_grad = carried
        index_rows, slot_counts, bag_ids, hot_rows, hot_bag_ids, bag_grad = item_data
        global_rows = (index_rows + offsets).reshape(-1).astype(jnp.int32)
        live_mask = (columns < slot_counts[:, None]).reshape(-1)
        pulled = lax.optimization_barrier(embedding_table[global_rows].astype(jnp.bfloat16))
        pulled = jnp.where(live_mask[:, None], pulled.astype(jnp.float32), 0.0)
        hot_pulled = hot_block[hot_rows].astype(jnp.float32)
        pooled = jax.ops.segment_sum(pulled, bag_ids, num_segments=B_DEV)
        pooled = pooled + jax.ops.segment_sum(hot_pulled, hot_bag_ids, num_segments=B_DEV)
        slot_grad = jnp.where(live_mask[:, None], bag_grad[bag_ids].astype(jnp.float32), 0.0)
        dense_grad = dense_grad.at[global_rows].add(slot_grad)
        hot_grad = hot_grad.at[hot_rows].add(bag_grad[hot_bag_ids].astype(jnp.float32))
        return ((dense_grad, hot_grad), pooled.astype(jnp.bfloat16))
    initial = (jnp.zeros((SHARDS * ROWS_DEV, D), jnp.float32), jnp.zeros((HOT, D), jnp.float32))
    (dense_grad, hot_grad), pooled = lax.scan(visit, initial, item_list)
    next_table, next_history = adagrad_rows(embedding_table, row_history, dense_grad)
    owner_history = lax.dynamic_slice_in_dim(hot_history, owner_start, HOT, 0)
    hot_updated, history_updated = adagrad_rows(owner_rows, owner_history, hot_grad)
    next_hot = lax.dynamic_update_slice_in_dim(hot_table, hot_updated, owner_start, 0)
    next_squares = lax.dynamic_update_slice_in_dim(hot_history, history_updated, owner_start, 0)
    return (pooled.reshape(REPLICAS, SHARDS * B_DEV, D), next_table, next_history, next_hot, next_squares)
```

```python
import functools

import jax
import jax.numpy as jnp
from jax import lax
from jax.experimental import pallas as pl
from jax.experimental.pallas import tpu as pltpu
from jax.sharding import PartitionSpec as P

learn_rate = 0.1
epsilon = 1e-08
LO = 256
GROUP = 4
bf16 = jnp.bfloat16
f32 = jnp.float32


def row_iota(n, m):
    return lax.broadcasted_iota(jnp.int32, (n, m), 0)


def onehot_rows(n, ids):
    return jnp.where(row_iota(n, ids.shape[1]) == ids, 1.0, 0.0).astype(bf16)


def code_parts(code):
    bag = jnp.where(code < 0, -1, code & (LO - 1))
    return code >> 16, (code >> 8) & (LO - 1), bag


def fold_table(table_ref, folded, high):
    width = table_ref.shape[1]
    for h in range(high):
        folded[h * width : (h + 1) * width, :] = table_ref[h * LO : (h + 1) * LO, :].astype(f32).T.astype(bf16)


def fetch(folded, code, high):
    width = folded.shape[0] // high
    hi, lo, bag = code_parts(code)
    every = jnp.dot(folded[...], onehot_rows(LO, lo), preferred_element_type=f32)
    picked = jnp.zeros((width, code.shape[1]), f32)
    for h in range(high):
        picked = jnp.where(hi == h, every[h * width : (h + 1) * width], picked)
    return picked.astype(bf16)


def pool(code, columns, bag_count):
    bag = code_parts(code)[2]
    return lax.dot_general(onehot_rows(bag_count, bag), columns, (((1,), (1,)), ((), ())), preferred_element_type=f32)


def scatter_terms(code, grad, high):
    hi, lo, bag = code_parts(code)
    spread = jnp.dot(grad, onehot_rows(grad.shape[1], bag), preferred_element_type=f32)
    parts = [jnp.where(hi == h, spread, 0.0).astype(bf16) for h in range(high)]
    return jnp.concatenate(parts, axis=0), onehot_rows(LO, lo)


def unfold(total, out_ref, high):
    width = out_ref.shape[1]
    for h in range(high):
        out_ref[h * LO : (h + 1) * LO, :] = total[h * width : (h + 1) * width, :].T.astype(out_ref.dtype)


def gather_kernel(high, code_ref, table_ref, out_ref, folded):
    @pl.when(pl.program_id(0) == 0)
    def _():
        fold_table(table_ref, folded, high)

    for k in range(GROUP):
        out_ref[k] = fetch(folded, code_ref[0, k : k + 1, :], high)


def gather_rows(codes, table):
    lists, slots = codes.shape
    rows, width = table.shape
    high = rows // LO
    return pl.pallas_call(
        functools.partial(gather_kernel, high),
        grid=(lists // GROUP,),
        in_specs=[
            pl.BlockSpec((1, GROUP, slots), lambda i: (i, 0, 0)),
            pl.BlockSpec((rows, width), lambda i: (0, 0)),
        ],
        out_specs=pl.BlockSpec((GROUP, width, slots), lambda i: (i, 0, 0)),
        out_shape=jax.ShapeDtypeStruct((lists, width, slots), bf16),
        scratch_shapes=[pltpu.VMEM((high * width, LO), bf16)],
        cost_estimate=pl.CostEstimate(flops=2 * lists * slots * rows * width, bytes_accessed=6 << 20, transcendentals=0),
        name="gather_rows",
    )(codes.reshape(lists // GROUP, GROUP, slots), table)


def pool_kernel(code_ref, columns_ref, start_ref, out_ref, total):
    step = pl.program_id(0)

    @pl.when(step == 0)
    def _():
        total[...] = start_ref[...]

    partial = pool(code_ref[0, 0:1, :], columns_ref[0], total.shape[0])
    for k in range(1, GROUP):
        partial = partial + pool(code_ref[0, k : k + 1, :], columns_ref[k], total.shape[0])
    total[...] += partial

    @pl.when(step == pl.num_programs(0) - 1)
    def _():
        out_ref[...] = total[...].astype(out_ref.dtype)


def pool_rows(codes, columns, start):
    lists, width, slots = columns.shape
    bags = start.shape[0]
    return pl.pallas_call(
        pool_kernel,
        grid=(lists // GROUP,),
        in_specs=[
            pl.BlockSpec((1, GROUP, slots), lambda i: (i, 0, 0)),
            pl.BlockSpec((GROUP, width, slots), lambda i: (i, 0, 0)),
            pl.BlockSpec((bags, width), lambda i: (0, 0)),
        ],
        out_specs=pl.BlockSpec((bags, width), lambda i: (0, 0)),
        out_shape=jax.ShapeDtypeStruct((bags, width), bf16),
        scratch_shapes=[pltpu.VMEM((bags, width), f32)],
        cost_estimate=pl.CostEstimate(flops=2 * lists * slots * bags * width, bytes_accessed=5 << 20, transcendentals=0),
        name="pool_rows",
    )(codes.reshape(lists // GROUP, GROUP, slots), columns, start)


def rowgrad_kernel(high, place_ref, code_ref, grad_ref, out_ref, total):
    step = pl.program_id(0)

    @pl.when(step == 0)
    def _():
        total[...] = jnp.zeros_like(total)

    terms, lows = [], []
    for k in range(GROUP):
        a, b = scatter_terms(code_ref[pl.ds(place_ref[step * GROUP + k], 1), :], grad_ref[k], high)
        terms.append(a)
        lows.append(b)
    total[...] += lax.dot_general(
        jnp.concatenate(terms, axis=1), jnp.concatenate(lows, axis=1), (((1,), (1,)), ((), ())), preferred_element_type=f32
    )

    @pl.when(step == pl.num_programs(0) - 1)
    def _():
        unfold(total, out_ref, high)


def row_gradients(place, codes, grads, rows):
    lists, slots = codes.shape
    _, width, bags = grads.shape
    high = rows // LO
    return pl.pallas_call(
        functools.partial(rowgrad_kernel, high),
        grid_spec=pltpu.PrefetchScalarGridSpec(
            num_scalar_prefetch=1,
            grid=(lists // GROUP,),
            in_specs=[
                pl.BlockSpec((lists, slots), lambda i, place: (0, 0)),
                pl.BlockSpec((GROUP, width, bags), lambda i, place: (i, 0, 0)),
            ],
            out_specs=pl.BlockSpec((rows, width), lambda i, place: (0, 0)),
            scratch_shapes=[pltpu.VMEM((high * width, LO), f32)],
        ),
        out_shape=jax.ShapeDtypeStruct((rows, width), bf16),
        cost_estimate=pl.CostEstimate(flops=2 * lists * slots * rows * width, bytes_accessed=5 << 20, transcendentals=0),
        name="row_gradients",
    )(place, codes, grads)


def hot_back_kernel(high, code_ref, grad_ref, out_ref, total):
    for k in range(code_ref.shape[0]):
        a, b = scatter_terms(code_ref[k : k + 1, :], grad_ref[...], high)
        part = lax.dot_general(a, b, (((1,), (1,)), ((), ())), preferred_element_type=f32)
        total[...] = part if k == 0 else total[...] + part
    unfold(total, out_ref, high)


def hot_gradients(codes, grad, rows):
    width = grad.shape[0]
    high = rows // LO
    return pl.pallas_call(
        functools.partial(hot_back_kernel, high),
        out_shape=jax.ShapeDtypeStruct((rows, width), bf16),
        scratch_shapes=[pltpu.VMEM((high * width, LO), f32)],
        cost_estimate=pl.CostEstimate(flops=2 * codes.size * rows * width, bytes_accessed=2 << 20, transcendentals=0),
        name="hot_gradients",
    )(codes, grad)


def hot_pool_kernel(high, code_ref, table_ref, out_ref, folded):
    fold_table(table_ref, folded, high)
    total = jnp.zeros(out_ref.shape, f32)
    for k in range(code_ref.shape[0]):
        code = code_ref[k : k + 1, :]
        total = total + pool(code, fetch(folded, code, high), out_ref.shape[0])
    out_ref[...] = total


def hot_pool(codes, table, bags):
    rows, width = table.shape
    high = rows // LO
    return pl.pallas_call(
        functools.partial(hot_pool_kernel, high),
        out_shape=jax.ShapeDtypeStruct((bags, width), f32),
        scratch_shapes=[pltpu.VMEM((high * width, LO), bf16)],
        cost_estimate=pl.CostEstimate(flops=2 * codes.size * rows * width, bytes_accessed=2 << 20, transcendentals=0),
        name="hot_pool",
    )(codes, table)


def exchange(x, axis):
    return lax.all_to_all(x, axis, split_axis=0, concat_axis=0, tiled=True)


def spread(x, axis, count):
    return exchange(jnp.broadcast_to(x[None], (count,) + x.shape), axis)


def adagrad_rows(weights, history, gradient):
    updated = history + jnp.mean(gradient * gradient, axis=1)
    return (weights - learn_rate * gradient / (jnp.sqrt(updated)[:, None] + epsilon), updated)


SIZE_Y, SIZE_Z, SIZE_C = 4, 8, 2


def shifted(dy, dz, dc):
    pairs = []
    for i in range(SIZE_Y * SIZE_Z * SIZE_C):
        y, z, c = i // (SIZE_Z * SIZE_C), i // SIZE_C % SIZE_Z, i % SIZE_C
        j = ((y + dy) % SIZE_Y * SIZE_Z + (z + dz) % SIZE_Z) * SIZE_C + (c + dc) % SIZE_C
        pairs.append((i, j))
    return pairs


def gather_grads(grad):
    along = jnp.stack([grad] + [lax.ppermute(grad, "table", shifted(0, s, 0)) for s in range(1, SIZE_Z)])
    plane = jnp.concatenate([along] + [lax.ppermute(along, "table", shifted(s, 0, 0)) for s in range(1, SIZE_Y)])
    return jnp.concatenate([plane, lax.ppermute(plane, "table", shifted(0, 0, 1))])


def sources():
    me = lax.axis_index("table")
    y, z, c = me // (SIZE_Z * SIZE_C), me // SIZE_C % SIZE_Z, me % SIZE_C
    k = jnp.arange(SIZE_Y * SIZE_Z * SIZE_C, dtype=jnp.int32)
    ky, kz, kc = k // SIZE_Z % SIZE_Y, k % SIZE_Z, k // (SIZE_Y * SIZE_Z)
    return ((y - ky) % SIZE_Y * SIZE_Z + (z - kz) % SIZE_Z) * SIZE_C + (c - kc) % SIZE_C


def shards(
    embedding_table,
    row_history,
    hot_table,
    hot_history,
    hot_owner,
    cold_index,
    cold_counts,
    cold_bags,
    hot_index,
    hot_bags,
    pooled_grad,
):
    peers = lax.axis_size("table")
    replicas = lax.axis_size("rep")
    rep = lax.axis_index("rep")
    hot_rows, width = hot_table.shape
    slots = cold_index.shape[2]
    bags = pooled_grad.shape[1]
    owner = hot_owner[0]

    live = jnp.arange(slots, dtype=jnp.int32)[None, :] < cold_counts[0][:, None]
    codes = jnp.where(live, cold_index[0] * LO + cold_bags[0], -1)
    hot_codes = (hot_index[0] * LO + hot_bags[0]).reshape(-1, LO)
    grad = pooled_grad[0].T

    asked = exchange(codes, "table")

    quarter = hot_rows // replicas
    piece = quarter // peers
    mine = lax.dynamic_slice_in_dim(hot_table, rep * quarter, quarter, 0).astype(bf16)
    pieces = exchange(mine.reshape(peers, piece, width), "table")
    own_piece = lax.dynamic_index_in_dim(pieces, owner, 0, keepdims=False)

    grads = gather_grads(grad)
    served = gather_rows(asked, embedding_table)
    pulled = exchange(served, "table")

    hot_quarter = spread(own_piece, "table", peers).reshape(quarter, width)
    hot_block = spread(hot_quarter, "rep", replicas).reshape(hot_rows, width)

    hot_part = hot_gradients(hot_codes, grad, hot_rows)
    by_replica = exchange(hot_part.reshape(replicas, quarter, width), "rep")
    quarter_sum = jnp.sum(by_replica.astype(f32), axis=0).astype(bf16)
    by_peer = exchange(quarter_sum.reshape(peers, piece, width), "table")
    piece_sum = jnp.sum(by_peer.astype(f32), axis=0)
    quarter_total = spread(piece_sum, "table", peers).reshape(quarter, width)
    hot_total = spread(quarter_total, "rep", replicas).reshape(hot_rows, width)

    dense = row_gradients(sources(), asked, grads, embedding_table.shape[0])
    ring = [[(i, (i + s) % replicas) for i in range(replicas)] for s in range(replicas)]
    total = dense.astype(f32)
    for s in range(1, replicas):
        total = total + lax.ppermute(dense, "rep", ring[s]).astype(f32)
    next_table, next_history = adagrad_rows(embedding_table, row_history, total)

    hot_updated, history_updated = adagrad_rows(hot_table, hot_history, hot_total)
    is_owner = lax.axis_index("table") == owner
    next_hot = jnp.where(is_owner, hot_updated, hot_table)
    next_squares = jnp.where(is_owner, history_updated, hot_history)

    hot_sum = hot_pool(hot_codes, hot_block, bags)
    pooled = pool_rows(codes, pulled, hot_sum)
    return (pooled[None], next_table, next_history, next_hot, next_squares)


def solution(mesh):
    in_specs = (
        P("table", None),
        P("table"),
        P("table", None),
        P("table"),
        P(),
        P("rep", "table", None),
        P("rep", "table"),
        P("rep", "table", None),
        P("rep", "table"),
        P("rep", "table"),
        P("rep", "table", None),
    )
    out_specs = (
        P("rep", "table", None),
        P("table", None),
        P("table"),
        P("table", None),
        P("table"),
    )
    return jax.shard_map(shards, mesh=mesh, in_specs=in_specs, out_specs=out_specs, check_vma=False)
```

```python
import functools

import jax
import jax.numpy as jnp
from jax import lax
from jax.experimental import pallas as pl
from jax.experimental.pallas import tpu as pltpu
from jax.sharding import PartitionSpec as P


learn_rate = 0.1
epsilon = 1e-08
LO = 256
GROUP = 8
bf16 = jnp.bfloat16
f32 = jnp.float32


def row_iota(n, m):
    return lax.broadcasted_iota(jnp.int32, (n, m), 0)


def onehot_rows(n, ids):
    return jnp.where(row_iota(n, ids.shape[1]) == ids, 1.0, 0.0).astype(bf16)


def code_parts(code):
    bag = jnp.where(code < 0, -1, code & (LO - 1))
    return code >> 16, (code >> 8) & (LO - 1), bag


def fold_table(table_ref, folded, high):
    width = table_ref.shape[1]
    for h in range(high):
        folded[h * width : (h + 1) * width, :] = table_ref[h * LO : (h + 1) * LO, :].astype(f32).T.astype(bf16)


def fetch(folded, code, high):
    width = folded.shape[0] // high
    hi, lo, _ = code_parts(code)
    every = jnp.dot(folded[...], onehot_rows(LO, lo), preferred_element_type=f32)
    picked = jnp.zeros((width, code.shape[1]), f32)
    for h in range(high):
        picked = jnp.where(hi == h, every[h * width : (h + 1) * width], picked)
    return picked.astype(bf16)


def pool(code, columns, bag_count):
    bag = code_parts(code)[2]
    return lax.dot_general(onehot_rows(bag_count, bag), columns, (((1,), (1,)), ((), ())), preferred_element_type=f32)


def scatter_terms(code, grad, high):
    hi, lo, bag = code_parts(code)
    spread_ = jnp.dot(grad, onehot_rows(grad.shape[1], bag), preferred_element_type=f32)
    parts = [jnp.where(hi == h, spread_, 0.0).astype(bf16) for h in range(high)]
    return jnp.concatenate(parts, axis=0), onehot_rows(LO, lo)


def unfold(total, out_ref, high):
    width = out_ref.shape[1]
    for h in range(high):
        out_ref[h * LO : (h + 1) * LO, :] = total[h * width : (h + 1) * width, :].T.astype(out_ref.dtype)


def gather_kernel(high, code_ref, table_ref, out_ref, folded):
    @pl.when(pl.program_id(0) == 0)
    def _():
        fold_table(table_ref, folded, high)

    for k in range(GROUP):
        out_ref[k] = fetch(folded, code_ref[0, k : k + 1, :], high)


def gather_rows(codes, table):
    lists, slots = codes.shape
    rows, width = table.shape
    high = rows // LO
    return pl.pallas_call(
        functools.partial(gather_kernel, high),
        grid=(lists // GROUP,),
        in_specs=[
            pl.BlockSpec((1, GROUP, slots), lambda i: (i, 0, 0)),
            pl.BlockSpec((rows, width), lambda i: (0, 0)),
        ],
        out_specs=pl.BlockSpec((GROUP, width, slots), lambda i: (i, 0, 0)),
        out_shape=jax.ShapeDtypeStruct((lists, width, slots), bf16),
        scratch_shapes=[pltpu.VMEM((high * width, LO), bf16)],
        cost_estimate=pl.CostEstimate(flops=2 * lists * slots * rows * width, bytes_accessed=6 << 20, transcendentals=0),
        name="gather_rows",
    )(codes.reshape(lists // GROUP, GROUP, slots), table)


def pool_kernel(code_ref, columns_ref, start_ref, out_ref, total):
    step = pl.program_id(0)

    @pl.when(step == 0)
    def _():
        total[...] = start_ref[...]

    partial = pool(code_ref[0, 0:1, :], columns_ref[0], total.shape[0])
    for k in range(1, GROUP):
        partial = partial + pool(code_ref[0, k : k + 1, :], columns_ref[k], total.shape[0])
    total[...] += partial

    @pl.when(step == pl.num_programs(0) - 1)
    def _():
        out_ref[...] = total[...].astype(out_ref.dtype)


def pool_rows(codes, columns, start):
    lists, width, slots = columns.shape
    bags = start.shape[0]
    return pl.pallas_call(
        pool_kernel,
        grid=(lists // GROUP,),
        in_specs=[
            pl.BlockSpec((1, GROUP, slots), lambda i: (i, 0, 0)),
            pl.BlockSpec((GROUP, width, slots), lambda i: (i, 0, 0)),
            pl.BlockSpec((bags, width), lambda i: (0, 0)),
        ],
        out_specs=pl.BlockSpec((bags, width), lambda i: (0, 0)),
        out_shape=jax.ShapeDtypeStruct((bags, width), bf16),
        scratch_shapes=[pltpu.VMEM((bags, width), f32)],
        cost_estimate=pl.CostEstimate(flops=2 * lists * slots * bags * width, bytes_accessed=5 << 20, transcendentals=0),
        name="pool_rows",
    )(codes.reshape(lists // GROUP, GROUP, slots), columns, start)


def rowgrad_kernel(high, place_ref, code_ref, grad_ref, out_ref, total):
    step = pl.program_id(0)

    @pl.when(step == 0)
    def _():
        total[...] = jnp.zeros_like(total)

    terms, lows = [], []
    for k in range(GROUP):
        a, b = scatter_terms(code_ref[pl.ds(place_ref[step * GROUP + k], 1), :], grad_ref[k], high)
        terms.append(a)
        lows.append(b)
    total[...] += lax.dot_general(
        jnp.concatenate(terms, axis=1), jnp.concatenate(lows, axis=1), (((1,), (1,)), ((), ())), preferred_element_type=f32
    )

    @pl.when(step == pl.num_programs(0) - 1)
    def _():
        unfold(total, out_ref, high)


def row_gradients(place, codes, grads, rows):
    lists, slots = codes.shape
    _, width, bags = grads.shape
    high = rows // LO
    return pl.pallas_call(
        functools.partial(rowgrad_kernel, high),
        grid_spec=pltpu.PrefetchScalarGridSpec(
            num_scalar_prefetch=1,
            grid=(lists // GROUP,),
            in_specs=[
                pl.BlockSpec((lists, slots), lambda i, place: (0, 0)),
                pl.BlockSpec((GROUP, width, bags), lambda i, place: (i, 0, 0)),
            ],
            out_specs=pl.BlockSpec((rows, width), lambda i, place: (0, 0)),
            scratch_shapes=[pltpu.VMEM((high * width, LO), f32)],
        ),
        out_shape=jax.ShapeDtypeStruct((rows, width), bf16),
        cost_estimate=pl.CostEstimate(flops=2 * lists * slots * rows * width, bytes_accessed=5 << 20, transcendentals=0),
        name="row_gradients",
    )(place, codes, grads)


def hot_back_kernel(high, code_ref, grad_ref, out_ref, total):
    for k in range(code_ref.shape[0]):
        a, b = scatter_terms(code_ref[k : k + 1, :], grad_ref[...], high)
        part = lax.dot_general(a, b, (((1,), (1,)), ((), ())), preferred_element_type=f32)
        total[...] = part if k == 0 else total[...] + part
    unfold(total, out_ref, high)


def hot_gradients(codes, grad, rows):
    width = grad.shape[0]
    high = rows // LO
    return pl.pallas_call(
        functools.partial(hot_back_kernel, high),
        out_shape=jax.ShapeDtypeStruct((rows, width), bf16),
        scratch_shapes=[pltpu.VMEM((high * width, LO), f32)],
        cost_estimate=pl.CostEstimate(flops=2 * codes.size * rows * width, bytes_accessed=2 << 20, transcendentals=0),
        name="hot_gradients",
    )(codes, grad)


def hot_pool_kernel(high, code_ref, table_ref, out_ref, folded):
    fold_table(table_ref, folded, high)
    total = jnp.zeros(out_ref.shape, f32)
    for k in range(code_ref.shape[0]):
        code = code_ref[k : k + 1, :]
        total = total + pool(code, fetch(folded, code, high), out_ref.shape[0])
    out_ref[...] = total


def hot_pool(codes, table, bags):
    rows, width = table.shape
    high = rows // LO
    return pl.pallas_call(
        functools.partial(hot_pool_kernel, high),
        out_shape=jax.ShapeDtypeStruct((bags, width), f32),
        scratch_shapes=[pltpu.VMEM((high * width, LO), bf16)],
        cost_estimate=pl.CostEstimate(flops=2 * codes.size * rows * width, bytes_accessed=2 << 20, transcendentals=0),
        name="hot_pool",
    )(codes, table)


def exchange(x, axis):
    return lax.all_to_all(x, axis, split_axis=0, concat_axis=0, tiled=True)


def adagrad_rows(weights, history, gradient):
    updated = history + jnp.mean(gradient * gradient, axis=1)
    return (weights - learn_rate * gradient / (jnp.sqrt(updated)[:, None] + epsilon), updated)


SIZE_Y, SIZE_Z, SIZE_C = 4, 8, 2
PEERS = SIZE_Y * SIZE_Z * SIZE_C


def swap(x, mask):
    return lax.ppermute(x, "table", [(i, i ^ mask) for i in range(PEERS)])


def shift_y(x, step):
    pairs = [(i, (i + step * SIZE_Z * SIZE_C) % PEERS) for i in range(PEERS)]
    return lax.ppermute(x, "table", pairs)


def turn(x, step, count):
    return lax.ppermute(x, "rep", [(i, (i + step) % count) for i in range(count)])


def for_devices(x, piece):
    split = x.reshape(SIZE_C, SIZE_Y, SIZE_Z, piece, x.shape[1])
    return split.transpose(1, 2, 0, 3, 4).reshape(PEERS, piece, x.shape[1])


def along_z(grad):
    along = grad[None]
    for mask in (8, 4, 2):
        along = jnp.concatenate([along, swap(along, mask)])
    return along


def beyond_z(along):
    plane = jnp.concatenate([along] + [shift_y(along, s) for s in range(1, SIZE_Y)])
    return jnp.concatenate([plane, swap(plane, 1)])


def sources():
    me = lax.axis_index("table")
    y, z, c = me // (SIZE_Z * SIZE_C), me // SIZE_C % SIZE_Z, me % SIZE_C
    k = jnp.arange(PEERS, dtype=jnp.int32)
    ky, kz, kc = k // SIZE_Z % SIZE_Y, k % SIZE_Z, k // (SIZE_Y * SIZE_Z)
    kz = (kz & 1) * 4 + (kz & 2) + (kz >> 2)
    return ((y - ky) % SIZE_Y * SIZE_Z + (z ^ kz)) * SIZE_C + (c ^ kc)


def doubled(x, masks):
    me = lax.axis_index("table")
    for mask in masks:
        upper = (me & mask) != 0
        other = swap(x, mask)
        x = jnp.concatenate([jnp.where(upper, other, x), jnp.where(upper, x, other)])
    return x


def by_replica(own, rep, count):
    parts = jnp.stack([own] + [turn(own, s, count) for s in range(1, count)])
    return jnp.concatenate([lax.dynamic_index_in_dim(parts, (rep - q) % count, 0, keepdims=False) for q in range(count)])


def step(
    embedding_table,
    row_history,
    hot_table,
    hot_history,
    hot_owner,
    cold_index,
    cold_counts,
    cold_bags,
    hot_index,
    hot_bags,
    pooled_grad,
):
    replicas = lax.axis_size("rep")
    rep = lax.axis_index("rep")
    hot_rows, width = hot_table.shape
    slots = cold_index.shape[2]
    bags = pooled_grad.shape[1]
    owner = hot_owner[0]

    live = jnp.arange(slots, dtype=jnp.int32)[None, :] < cold_counts[0][:, None]
    codes = jnp.where(live, cold_index[0] * LO + cold_bags[0], -1)
    hot_codes = (hot_index[0] * LO + hot_bags[0]).reshape(-1, LO)
    grad = pooled_grad[0].T

    asked = exchange(codes, "table")
    is_owner = lax.axis_index("table") == owner
    quarter = hot_rows // replicas
    piece = quarter // PEERS

    hot_part = hot_gradients(hot_codes, grad, hot_rows)
    hot_part = hot_part.reshape(replicas, quarter, width)
    quarter_sum = lax.dynamic_index_in_dim(hot_part, rep, 0, keepdims=False).astype(f32)
    for s in range(1, replicas):
        part = lax.dynamic_index_in_dim(hot_part, (rep + s) % replicas, 0, keepdims=False)
        quarter_sum = quarter_sum + turn(part, s, replicas).astype(f32)
    mine = lax.dynamic_slice_in_dim(hot_table, rep * quarter, quarter, 0).astype(bf16)
    both = jnp.concatenate([for_devices(quarter_sum.astype(bf16), piece), for_devices(mine, piece)], axis=1)
    pieces = exchange(both, "table")
    piece_sum = jnp.sum(pieces[:, :piece].astype(f32), axis=0)
    own_piece = lax.dynamic_index_in_dim(pieces, owner, 0, keepdims=False)[piece:].astype(f32)

    along = along_z(grad)
    served = gather_rows(asked, embedding_table)
    hot_both = doubled(jnp.stack([piece_sum, own_piece])[None], (2, 4, 8))
    served, along, hot_both = lax.optimization_barrier((served, along, hot_both))
    pulled = exchange(served, "table")

    grads = beyond_z(along)
    hot_both = doubled(hot_both, (16, 32, 1))
    quarter_total = hot_both[:, 0].reshape(quarter, width)
    quarter_block = hot_both[:, 1].reshape(quarter, width).astype(bf16)
    hot_block = jnp.concatenate([quarter_block] + [turn(quarter_block, s, replicas) for s in range(1, replicas)])
    hot_total = by_replica(quarter_total, rep, replicas)
    hot_row = hot_codes >> 8
    hot_place = (rep - hot_row // quarter) % replicas * quarter + hot_row % quarter
    block_codes = (hot_place << 8) | (hot_codes & 255)

    dense = row_gradients(sources(), asked, grads, embedding_table.shape[0])
    total = dense.astype(f32)
    for s in range(1, replicas):
        total = total + turn(dense, s, replicas).astype(f32)
    next_table, next_history = adagrad_rows(embedding_table, row_history, total)

    hot_updated, history_updated = adagrad_rows(hot_table, hot_history, hot_total)
    next_hot = jnp.where(is_owner, hot_updated, hot_table)
    next_squares = jnp.where(is_owner, history_updated, hot_history)

    hot_sum = hot_pool(block_codes, hot_block, bags)
    pooled = pool_rows(codes, pulled, hot_sum)
    return (pooled[None], next_table, next_history, next_hot, next_squares)


def solution(mesh):
    in_specs = (
        P("table", None),
        P("table"),
        P("table", None),
        P("table"),
        P(),
        P("rep", "table", None),
        P("rep", "table"),
        P("rep", "table", None),
        P("rep", "table"),
        P("rep", "table"),
        P("rep", "table", None),
    )
    out_specs = (
        P("rep", "table", None),
        P("table", None),
        P("table"),
        P("table", None),
        P("table"),
    )
    return jax.shard_map(step, mesh=mesh, in_specs=in_specs, out_specs=out_specs, check_vma=False)
```
